128 devices in a mesh: ka: 16 (over x, y), ta: 8 (over z, core).
Axes of the slice: x: 4, y: 4, z: 4, core: 2. Of those that a mesh axis runs over, the one named last changes fastest.
Arguments:
- green: float32 [2, 256, 512, 128], P(None, 'ka', 'ta'), may hold values from -3 to 3
- energies: float32 [256], P('ka'), may hold values from -2 to 2
- reach: int32 [512], P('ta'), may hold values from 1 to 128, as said below
Outputs:
- evolved: float32 [2, 256, 512, 128], P(None, 'ka', 'ta')
The draws below stay inside these ranges and needn't reach their ends.
Inputs may be any that keep to these rules, and one draw needn't show every extreme that they name: `reach`: at least one time reaches 128.
All inputs are finite; a program needn't handle non-finite values.
Results may differ from the reference program's by a relative error of at most 0.0013.
Values may be sent and summed in bfloat16 or wider, within the bound.
No kernel may reach another device: no remote copies, remote signals or barrier semaphores. Data moves between devices by JAX's collectives and lax.ppermute only.
A program may use at most 128 MiB of HBM per device.

```python
import math
import jax
import jax.numpy as jnp
from jax import lax

K = 256
MEM = 128
TPAN = 64
NT = 512


def draw_reach(key, part):
    first_key = jax.random.fold_in(key, 11)
    second_key = jax.random.fold_in(key, 12)
    values = jax.random.randint(first_key, (NT,), 1, MEM + 1, dtype=jnp.int32)
    where_full = jax.random.randint(second_key, (), 0, NT, dtype=jnp.int32)
    return values.at[where_full].set(MEM)


def block_scale(key, extent, split, least, largest):
    loudness = 1.0
    for dim, blocks in split:
        draws = jax.random.uniform(jax.random.fold_in(jax.random.fold_in(key, 6), dim), (blocks,), jnp.float32, least / len(split), largest / len(split))
        loudness = loudness * jnp.repeat(jnp.exp(draws), extent[dim] // blocks).reshape((-1,) + (1,) * (len(extent) - 1 - dim))
    return loudness


def normal_values(stream_key, extent, spread, most, split=(), held_as=jnp.bfloat16):
    level = block_scale(stream_key, extent, split, -0.22, 0.18) if split else 1.0
    array = jax.random.normal(stream_key, extent, jnp.float32) * spread * level
    return jnp.minimum(jnp.maximum(array, -most), most).astype(held_as)


def setup_inputs(seed: int = 0) -> dict:
    keys = jax.random.split(jax.random.key(seed), 4)
    green = normal_values(keys[0], (2, K, NT, MEM), 0.5, 3.0, ((1, 16), (2, 8)), jnp.float32)
    energies = jnp.clip(jax.random.uniform(keys[1], (K,), jnp.float32, -2.0, 2.0) * block_scale(keys[1], (K,), ((0, 16),), -0.4, 0.0), -2.0, 2.0)
    reach = draw_reach(jax.random.fold_in(keys[3], 71), 0)
    return {"green": green, "energies": energies, "reach": reach}


coupling = 1.0
quadrature = 0.0625
step_size = 0.25

def tables(count):
    numbers = jnp.arange(count, dtype=jnp.int32)
    turns = (numbers[:, None] * numbers[None, :] % count).astype(jnp.float32)
    phase = turns * (2.0 * math.pi / count)
    scaling = 1.0 / math.sqrt(count)
    cosines = jnp.cos(phase) * scaling
    sines = jnp.sin(phase) * scaling
    forward = jnp.stack([jnp.stack([cosines, -sines]), jnp.stack([sines, cosines])]).astype(jnp.bfloat16)
    inverse = jnp.stack([jnp.stack([cosines, sines]), jnp.stack([-sines, cosines])]).astype(jnp.bfloat16)
    return (forward, inverse)

def skew_band(band_vals):
    row_count, lag_count = (band_vals.shape[-2], band_vals.shape[-1])
    leading = band_vals.shape[:-2]
    flipped = jnp.flip(band_vals, -1)
    padded = jnp.pad(flipped, [(0, 0)] * len(leading) + [(0, 0), (0, row_count)])
    flattened = padded.reshape(leading + (row_count * (lag_count + row_count),))
    flattened = flattened[..., :row_count * (lag_count + row_count - 1)]
    return flattened.reshape(leading + (row_count, lag_count + row_count - 1))

def unskew_band(dense_vals, lag_count):
    row_count, span_all = (dense_vals.shape[-2], dense_vals.shape[-1])
    leading = dense_vals.shape[:-2]
    flattened = dense_vals.reshape(leading + (row_count * span_all,))
    flattened = jnp.pad(flattened, [(0, 0)] * len(leading) + [(0, row_count)])
    squared = flattened.reshape(leading + (row_count, span_all + 1))
    return jnp.flip(squared[..., :lag_count], -1)

def self_energy(rounded, forward, inverse):
    real_space = jnp.einsum('acrk,cktl->artl', forward.astype(jnp.float32), rounded.astype(jnp.float32), precision=lax.Precision.HIGHEST)
    weight = real_space[0] * real_space[0] + real_space[1] * real_space[1]
    local_sigma = (-coupling * weight[None] * real_space).astype(jnp.bfloat16)
    sigma_k = jnp.einsum('ackr,crtl->aktl', inverse.astype(jnp.float32), local_sigma.astype(jnp.float32), precision=lax.Precision.HIGHEST)
    return sigma_k.astype(jnp.bfloat16)

def mask_reach(sigma_k, reach_part):
    lag_index = jnp.arange(sigma_k.shape[-1], dtype=jnp.int32)
    keeping = lag_index[None, :] < reach_part[:, None]
    return jnp.where(keeping[None, None], sigma_k, jnp.zeros((), jnp.bfloat16))

def collision(sigma_k, history):
    lag_count = sigma_k.shape[-1]
    left_dense = skew_band(sigma_k).astype(jnp.float32)
    right_dense = skew_band(history)[..., lag_count - 1:].astype(jnp.float32)
    left_blocks = jnp.stack([jnp.stack([left_dense[0], -left_dense[1]], 2), jnp.stack([left_dense[1], left_dense[0]], 2)])
    product = jnp.einsum('akrcu,ckus->akrs', left_blocks, right_dense, precision=lax.Precision.HIGHEST)
    return quadrature * unskew_band(product, lag_count)

def rate_of(state_now, energies, collide):
    energy_col = energies[:, None, None]
    return jnp.stack([energy_col * state_now[1] + collide[1], -(energy_col * state_now[0] + collide[0])])

def evaluate(state_now, energies, reach, forward, inverse):
    rounded = state_now.astype(jnp.bfloat16)
    momenta, time_count, lag_count = (rounded.shape[1], rounded.shape[2], rounded.shape[3])
    padded = jnp.pad(rounded, ((0, 0), (0, 0), (lag_count - 1, 0), (0, 0)))
    panel_count = time_count // TPAN

    def one_panel(panel_index):
        first_row = (panel_index * TPAN).astype(jnp.int32)
        own_rows = lax.dynamic_slice_in_dim(rounded, first_row, TPAN, 2)
        sigma_k = self_energy(own_rows, forward, inverse)
        reach_part = lax.dynamic_slice_in_dim(reach, first_row, TPAN, 0)
        sigma_k = mask_reach(sigma_k, reach_part)
        history = lax.dynamic_slice_in_dim(padded, first_row, lag_count - 1 + TPAN, 2)
        return collision(sigma_k, history)
    pieces = lax.map(one_panel, jnp.arange(panel_count, dtype=jnp.int32))
    collide = jnp.moveaxis(pieces, 0, 2).reshape(2, momenta, time_count, lag_count)
    return rate_of(state_now, energies, collide)

def reference(green, energies, reach):
    forward, inverse = tables(K)
    state_now = green
    for counter in range(2):
        rate_now = evaluate(state_now, energies, reach, forward, inverse)
        predicted = state_now + step_size * rate_now
        rate_next = evaluate(predicted, energies, reach, forward, inverse)
        state_now = state_now + 0.5 * step_size * (rate_now + rate_next)
    return state_now
```

```python
import jax
import jax.numpy as jnp
import numpy as np
from jax import lax
from jax.experimental import pallas as pl
from jax.experimental.pallas import tpu as pltpu
from jax.sharding import PartitionSpec as P

K = 256
MEM = 128
ROWS = 64
OWN = 16
GROUP = 16
PART = 4
KB = 4

quadrature = 0.0625
step_size = 0.25

F32 = jnp.float32
BF16 = jnp.bfloat16


def tables(count):
    numbers = np.arange(count)
    phase = (numbers[:, None] * numbers[None, :] % count) * (2.0 * np.pi / count)
    both = np.concatenate([np.cos(phase), np.sin(phase)], 0) / np.sqrt(count)
    return jnp.asarray(both.astype(np.float32).astype(jnp.bfloat16))


def grids():
    row = lax.broadcasted_iota(jnp.int32, (ROWS, MEM), 0)
    lane = lax.broadcasted_iota(jnp.int32, (ROWS, MEM), 1)
    return row, lane


def pick(block, index):
    return jnp.take_along_axis(block, index, axis=1)


def lanes(block, index):
    pieces = [pick(block[i : i + 8], index[i : i + 8]) for i in range(0, ROWS, 8)]
    return jnp.concatenate(pieces, 0)


def half_turn(block):
    return pltpu.roll(block, MEM // 2, 1)


def self_energy_kernel(table, x, out):
    both = table[...]
    for pair in range(0, PART, 2):
        fields = []
        for part in range(2):
            sides = [x[:, part, pair + i].reshape(K, MEM) for i in range(2)]
            rhs = jnp.concatenate(sides, 1)
            fields.append(jnp.dot(both, rhs, preferred_element_type=F32))
        re = fields[0][:K] - fields[1][K:]
        im = fields[0][K:] + fields[1][:K]
        weight = -(re * re + im * im)
        zr = (weight * re).astype(BF16)
        zi = (weight * im).astype(BF16)
        a = jnp.dot(both, zr, preferred_element_type=F32)
        b = jnp.dot(both, zi, preferred_element_type=F32)
        sigma = ((a[:K] + b[K:]).astype(BF16), (b[:K] - a[K:]).astype(BF16))
        for part in range(2):
            for i in range(2):
                side = sigma[part][:, i * MEM : (i + 1) * MEM]
                out[:, part, pair + i] = side.reshape(GROUP, OWN, MEM)


def self_energy(table, spread):
    return pl.pallas_call(
        self_energy_kernel,
        out_shape=jax.ShapeDtypeStruct(spread.shape, BF16),
        name="self_energy",
    )(table, spread)


def emit(i, value, turned, low, near, far):
    row, lane = grids()
    turn = (lane + row) & (MEM - 1)
    wrap = lane + row >= MEM
    shifted = lane + row >= MEM // 2
    high = []
    for c in range(2):
        rounded = value[c].astype(BF16).astype(F32)
        k = pl.program_id(0) * KB + i
        turned[c, pl.ds(k, ROWS, stride=OWN), :] = rounded
        own = lanes(rounded, turn)
        low[c, i] = jnp.where(wrap, 0.0, own).astype(BF16)
        high.append(jnp.where(wrap, own, 0.0))
        near[c, i] = jnp.where(shifted, half_turn(own), 0.0).astype(BF16)
    far[i] = (high[0] + half_turn(high[1])).astype(BF16)


def flush(turned, chunk):
    @pl.when(pl.program_id(0) == pl.num_programs(0) - 1)
    def _():
        for d in range(GROUP):
            for c in range(2):
                for j in range(PART):
                    t = d * PART + j
                    chunk[d, c, j] = turned[c, t * OWN : (t + 1) * OWN, :].astype(BF16)


def prepare_kernel(x, low, near, far, chunk, turned):
    for i in range(KB):
        emit(i, (x[0, i], x[1, i]), turned, low, near, far)
    flush(turned, chunk)


def split_far(packed):
    row, lane = grids()
    upper = lane >= MEM // 2
    zero = jnp.zeros_like(packed)
    return jnp.where(upper, packed, zero), jnp.where(upper, half_turn(packed), zero)


def stage_kernel(first, last, energies, reach, sigma, low_in, far_own, near_in, far_in, x, *rest):
    if first:
        base = None
        ahead, out, low, near, far, chunk, held, turned = rest
    elif last:
        base, out, held = rest
    else:
        base, out, low, near, far, chunk, held, turned = rest

    row, lane = grids()

    @pl.when(pl.program_id(0) == 0)
    def _():
        part_lane = lax.broadcasted_iota(jnp.int32, (OWN, MEM), 1)
        for d in range(GROUP):
            for j in range(PART):
                t = d * PART + j
                keep = part_lane < reach[t]
                for c in range(2):
                    block = jnp.where(keep, sigma[d, c, j].astype(F32), 0.0)
                    held[c, t * OWN : (t + 1) * OWN, :] = block

    back = (row - lane) & (MEM - 1)
    own_side = (lane <= row) | (lane >= ROWS)
    far_side = (lane > row) & (lane < ROWS)
    turn = (lane - row) & (MEM - 1)
    inside = lane + row < MEM
    for i in range(KB):
        k = pl.program_id(0) * KB + i
        left = []
        for c in range(2):
            memory = lanes(held[c, pl.ds(k, ROWS, stride=OWN), :], back)
            left.append(
                jnp.concatenate(
                    [
                        jnp.where(own_side, memory, 0.0).astype(BF16),
                        jnp.where(far_side, memory, 0.0).astype(BF16),
                    ],
                    1,
                )
            )
        left = jnp.concatenate(left, 0)
        high = split_far(far_own[i])
        away = split_far(far_in[i])
        zero = jnp.zeros((ROWS, MEM), BF16)
        product = []
        for c in range(2):
            right = jnp.concatenate(
                [
                    jnp.concatenate([high[c], low_in[c, i]], 1),
                    jnp.concatenate([zero, near_in[c, i]], 1),
                    jnp.concatenate([zero, away[c]], 1),
                    jnp.concatenate([zero, zero], 1),
                ],
                0,
            )
            product.append(jnp.dot(left, right, preferred_element_type=F32))
        total = (
            product[0][:ROWS] - product[1][ROWS:],
            product[0][ROWS:] + product[1][:ROWS],
        )
        collide = []
        for c in range(2):
            chosen = jnp.where(inside, total[c][:, MEM:], total[c][:, :MEM])
            collide.append(quadrature * lanes(chosen, turn))
        energy = energies[k]
        xr, xi = x[0, i], x[1, i]
        rate = (energy * xi + collide[1], -(energy * xr + collide[0]))
        value = []
        for c in range(2):
            if first:
                here = x[c, i]
                ahead[c, i] = here + (0.5 * step_size) * rate[c]
                value.append(here + step_size * rate[c])
            else:
                value.append(base[c, i] + (0.5 * step_size) * rate[c])
            out[c, i] = value[c]
        if not last:
            emit(i, value, turned, low, near, far)
    if not last:
        flush(turned, chunk)


def specs():
    return dict(
        state=pl.BlockSpec((2, KB, ROWS, MEM), lambda g: (0, g, 0, 0)),
        far=pl.BlockSpec((KB, ROWS, MEM), lambda g: (g, 0, 0)),
        chunk=pl.BlockSpec((GROUP, 2, PART, OWN, MEM), lambda g: (0, 0, 0, 0, 0)),
        scalar=pl.BlockSpec(memory_space=pltpu.SMEM),
    )


def shapes():
    return dict(
        state=jax.ShapeDtypeStruct((2, OWN, ROWS, MEM), F32),
        rows=jax.ShapeDtypeStruct((2, OWN, ROWS, MEM), BF16),
        far=jax.ShapeDtypeStruct((OWN, ROWS, MEM), BF16),
        chunk=jax.ShapeDtypeStruct((GROUP, 2, PART, OWN, MEM), BF16),
    )


def prepare(x):
    spec, shape = specs(), shapes()
    return pl.pallas_call(
        prepare_kernel,
        grid=(OWN // KB,),
        in_specs=[spec["state"]],
        out_specs=[spec["state"], spec["state"], spec["far"], spec["chunk"]],
        out_shape=[shape["rows"], shape["rows"], shape["far"], shape["chunk"]],
        scratch_shapes=[pltpu.VMEM((2, ROWS * OWN, MEM), F32)],
        name="prepare",
    )(x)


def stage(first, last, energies, reach, sigma, history, x, base=None):
    spec, shape = specs(), shapes()
    state = spec["state"]
    in_specs = [spec["scalar"], spec["scalar"], spec["chunk"]]
    in_specs += [state, spec["far"], state, spec["far"], state]
    operands = [energies, reach, sigma, *history, x]
    if not first:
        in_specs.append(state)
        operands.append(base)
    out_specs, out_shape = [state], [shape["state"]]
    scratch = pltpu.VMEM((2, ROWS * OWN, MEM), F32)
    scratches = [scratch]
    if first:
        out_specs.append(state)
        out_shape.append(shape["state"])
    if not last:
        out_specs += [state, state, spec["far"], spec["chunk"]]
        out_shape += [shape["rows"], shape["rows"], shape["far"], shape["chunk"]]
        scratches.append(scratch)

    def kernel(*refs):
        stage_kernel(first, last, *refs)

    return pl.pallas_call(
        kernel,
        grid=(OWN // KB,),
        in_specs=in_specs,
        out_specs=out_specs,
        out_shape=out_shape,
        scratch_shapes=scratches,
        name="stage",
    )(*operands)


def from_behind(block, distance):
    count = lax.axis_size("ta")
    return lax.ppermute(block, "ta", [(i - distance, i) for i in range(distance, count)])


def exchange(block):
    return lax.all_to_all(block, "ka", split_axis=0, concat_axis=0, tiled=True)


def on_device(green, energies, reach):
    table = tables(K)

    def inputs(low, near, far, chunk):
        spread = exchange(chunk)
        history = (low, far, from_behind(near, 1), from_behind(far, 2))
        return exchange(self_energy(table, spread)), history

    x = green
    turned = prepare(x)
    for counter in range(2):
        sigma, history = inputs(*turned)
        ahead, guess, *turned = stage(True, False, energies, reach, sigma, history, x)
        sigma, history = inputs(*turned)
        if counter == 0:
            x, *turned = stage(False, False, energies, reach, sigma, history, guess, ahead)
        else:
            (x,) = stage(False, True, energies, reach, sigma, history, guess, ahead)
    return x


def solution(mesh):
    in_specs = (P(None, "ka", "ta", None), P("ka"), P("ta"))
    out_specs = P(None, "ka", "ta", None)
    return jax.shard_map(
        on_device, mesh=mesh, in_specs=in_specs, out_specs=out_specs, check_vma=False
    )
```

```python
import jax
import jax.numpy as jnp
import numpy as np
from jax import lax
from jax.experimental import pallas as pl
from jax.experimental.pallas import tpu as pltpu
from jax.sharding import PartitionSpec as P

K = 256
MEM = 128
ROWS = 64
OWN = 16
GROUP = 16
PART = 4
KB = 4
STEPS = OWN // KB
MIB = 2**20

quadrature = 0.0625
step_size = 0.25

F32 = jnp.float32
BF16 = jnp.bfloat16


def tables(count):
    numbers = np.arange(count)
    phase = (numbers[:, None] * numbers[None, :] % count) * (2.0 * np.pi / count)
    both = np.concatenate([np.cos(phase), np.sin(phase)], 0) / np.sqrt(count)
    return jnp.asarray(both.astype(np.float32).astype(jnp.bfloat16))


def grids():
    row = lax.broadcasted_iota(jnp.int32, (ROWS, MEM), 0)
    lane = lax.broadcasted_iota(jnp.int32, (ROWS, MEM), 1)
    return row, lane


def turn_over(block):
    row, lane = grids()
    index = (row - lane) & (MEM - 1)
    pieces = [
        jnp.take_along_axis(block[i : i + 8], index[i : i + 8], axis=1) for i in range(0, ROWS, 8)
    ]
    return jnp.concatenate(pieces, 0)


def half_turn(block):
    return pltpu.roll(block, MEM // 2, 1)


def self_energy_kernel(keep, table, x, out, y, sems):
    def save(pair):
        here = pl.ds(2 * pair, 2)
        return pltpu.make_async_copy(y.at[:, :, here], out.at[:, :, here], sems.at[pair])

    both = table[...]
    for pair in range(2):
        fields = []
        for part in range(2):
            sides = [x[:, part, 2 * pair + i].reshape(K, MEM) for i in range(2)]
            rhs = jnp.concatenate(sides, 1)
            fields.append(jnp.dot(both, rhs, preferred_element_type=F32))
        re = fields[0][:K] - fields[1][K:]
        im = fields[0][K:] + fields[1][:K]
        weight = -(re * re + im * im)
        zr = (weight * re).astype(BF16)
        zi = (weight * im).astype(BF16)
        a = jnp.dot(both, zr, preferred_element_type=F32)
        b = jnp.dot(both, zi, preferred_element_type=F32)
        sigma = (a[:K] + b[K:], b[:K] - a[K:])
        for part in range(2):
            for i in range(2):
                side = sigma[part][:, i * MEM : (i + 1) * MEM]
                kept = keep[2 * pair + i : 2 * pair + i + 1, :] > 0
                side = jnp.where(kept, side, 0.0).astype(BF16)
                y[:, part, 2 * pair + i] = side.reshape(GROUP, OWN, MEM)
        save(pair).start()
    for pair in range(2):
        save(pair).wait()


CHUNK = (GROUP, 2, PART, OWN, MEM)
STATE = (2, OWN, ROWS, MEM)
FAR = (OWN, ROWS, MEM)
HBM = pl.BlockSpec(memory_space=pltpu.HBM)
SMEM = pl.BlockSpec(memory_space=pltpu.SMEM)
VMEM = pl.BlockSpec(memory_space=pltpu.VMEM)


def params(mib):
    return pltpu.CompilerParams(vmem_limit_bytes=int(mib * MIB))


def self_energy(keep, table, spread):
    return pl.pallas_call(
        self_energy_kernel,
        in_specs=[VMEM, VMEM, VMEM],
        out_specs=HBM,
        out_shape=pltpu.HBM(CHUNK, BF16),
        scratch_shapes=[pltpu.VMEM(CHUNK, BF16), pltpu.SemaphoreType.DMA((2,))],
        compiler_params=params(12),
        name="self_energy",
    )(keep, table, spread)


def piece(ref, q):
    here = pl.ds(q * KB, KB)
    return ref.at[here] if len(ref.shape) == 3 else ref.at[:, here]


def mover(pairs, sems, first):
    def move(n, q):
        source, target = pairs[n]
        return pltpu.make_async_copy(piece(source, q), piece(target, q), sems.at[first + n, q])

    return move


def send_chunk(turned, block, chunk, sem):
    for d in range(GROUP):
        for c in range(2):
            for j in range(PART):
                t = d * PART + j
                block[d, c, j] = turned[c, t * OWN : (t + 1) * OWN, :].astype(BF16)
    copy = pltpu.make_async_copy(block, chunk, sem)
    copy.start()
    return copy


def emit(k, value, turned, near, far):
    row, lane = grids()
    causal = lane <= row
    low = []
    for c in range(2):
        turned[c, pl.ds(k, ROWS, stride=OWN), :] = value[c]
        near[c, k] = value[c].astype(BF16)
        low.append(jnp.where(causal, value[c], 0.0))
    far[k] = (low[0] + half_turn(low[1])).astype(BF16)


def prepare_kernel(x_in, out, near, far, chunk, x, y, turned, block, sems, sem):
    load = mover([(x_in, x)], sems, 0)
    pairs = [(y, out)]
    save = mover(pairs, sems, 1)
    for q in range(STEPS):
        load(0, q).start()

    def step(q, carry):
        load(0, q).wait()
        for i in range(KB):
            k = q * KB + i
            value = [turn_over(x[c, k]) for c in range(2)]
            for c in range(2):
                y[c, k] = value[c]
            emit(k, value, turned, near, far)
        return carry

    lax.fori_loop(0, STEPS, step, 0)
    last = send_chunk(turned, block, chunk, sem)
    for n in range(len(pairs)):
        for q in range(STEPS):
            save(n, q).start()
    for n in range(len(pairs)):
        for q in range(STEPS):
            save(n, q).wait()
    last.wait()


WIDE = pltpu.HBM(STATE, F32)
EMITTED = [pltpu.VMEM(STATE, BF16), pltpu.VMEM(FAR, BF16), pltpu.HBM(CHUNK, BF16)]


def emitting():
    return [
        pltpu.VMEM(STATE, BF16),
        pltpu.VMEM(FAR, BF16),
        pltpu.VMEM((2, ROWS * OWN, MEM), F32),
        pltpu.VMEM(CHUNK, BF16),
    ]


def prepare(x):
    scratch = pltpu.VMEM(STATE, F32)
    return pl.pallas_call(
        prepare_kernel,
        in_specs=[HBM],
        out_specs=[HBM, VMEM, VMEM, HBM],
        out_shape=[WIDE] + EMITTED,
        scratch_shapes=[scratch, scratch]
        + emitting()[2:]
        + [pltpu.SemaphoreType.DMA((2, STEPS)), pltpu.SemaphoreType.DMA],
        compiler_params=params(16),
        name="prepare",
    )(pltpu.with_memory_space_constraint(x, pltpu.HBM))


def stage_kernel(first, last, *refs):
    refs = list(refs)
    energies, sigma, own, own_low, near, far, base_in = refs[:7]
    if last:
        out, base, result, held, sems = refs[7:]
    else:
        out, mine, low, chunk, base, result, held, sems, turned, block, chunk_sem = refs[7:]

    loads = [(base_in, base)]
    saves = [(result, out)]
    load = mover(loads, sems, 0)
    save = mover(saves, sems, len(loads))
    for q in range(STEPS):
        for n in range(len(loads)):
            load(n, q).start()

    for d in range(GROUP):
        for c in range(2):
            for j in range(PART):
                t = d * PART + j
                held[c, t * OWN : (t + 1) * OWN, :] = sigma[d, c, j].astype(F32)

    row, lane = grids()
    causal = lane <= row
    own_side = causal | (lane >= ROWS)
    seen = lane <= row + ROWS
    lower = lane < ROWS

    def only(kept, block):
        return jnp.where(kept, block, jnp.zeros_like(block))

    def step(q, carry):
        for n in range(len(loads)):
            load(n, q).wait()
        for i in range(KB):
            k = q * KB + i
            left = []
            for c in range(2):
                memory = held[c, pl.ds(k, ROWS, stride=OWN), :]
                inner = jnp.where(own_side, memory, 0.0).astype(BF16)
                outer = jnp.where(own_side, 0.0, memory).astype(BF16)
                left.append(jnp.concatenate([inner, outer[:, :ROWS]], 1))
            left = jnp.concatenate(left, 0)
            packed = far[k]
            away = (packed, half_turn(packed))
            sides = []
            for c in range(2):
                rows = [
                    only(~causal, own[c, k]),
                    only(seen, half_turn(near[c, k])),
                    only(lower, away[c]),
                ]
                sides.append(jnp.concatenate(rows, 0))
            early = jnp.dot(left, jnp.concatenate(sides, 1), preferred_element_type=F32)
            late = jnp.dot(left[:, :ROWS], own_low[k], preferred_element_type=F32)
            collide = (
                jnp.where(
                    causal,
                    late[:ROWS] - half_turn(late[ROWS:]),
                    early[:ROWS, :MEM] - early[ROWS:, MEM:],
                ),
                jnp.where(
                    causal,
                    late[ROWS:] + half_turn(late[:ROWS]),
                    early[ROWS:, :MEM] + early[:ROWS, MEM:],
                ),
            )
            collide = [quadrature * part for part in collide]
            half = 0.5 * step_size
            if first:
                energy = energies[k]
                xr, xi = base[0, k], base[1, k]
                fr = energy * xi + collide[1]
                fi = -(energy * xr + collide[0])
                value = (xr + step_size * fr, xi + step_size * fi)
                result[0, k] = xr + half * (fr + energy * value[1])
                result[1, k] = xi + half * (fi - energy * value[0])
            else:
                value = (base[0, k] + half * collide[1], base[1, k] - half * collide[0])
                for c in range(2):
                    result[c, k] = turn_over(value[c]) if last else value[c]
            if not last:
                emit(k, value, turned, mine, low)
        for n in range(len(saves)):
            save(n, q).start()
        return carry

    lax.fori_loop(0, STEPS, step, 0)
    if not last:
        send_chunk(turned, block, chunk, chunk_sem).wait()
    for q in range(STEPS):
        for n in range(len(saves)):
            save(n, q).wait()


def stage(first, last, energies, sigma, own, own_low, near, far, base):
    state = pltpu.VMEM(STATE, F32)
    scratch = [state, state, pltpu.VMEM((2, ROWS * OWN, MEM), F32)]
    scratch += [pltpu.SemaphoreType.DMA((2, STEPS))]
    out_shape, spaces = [WIDE], [HBM]
    if not last:
        out_shape += EMITTED
        spaces += [VMEM, VMEM, HBM]
        scratch += emitting()[2:] + [pltpu.SemaphoreType.DMA]

    def kernel(*refs):
        stage_kernel(first, last, *refs)

    return pl.pallas_call(
        kernel,
        in_specs=[SMEM] + [VMEM] * 5 + [HBM],
        out_specs=spaces,
        out_shape=out_shape,
        scratch_shapes=scratch,
        compiler_params=params(16),
        name="stage",
    )(energies, sigma, own, own_low, near, far, pltpu.with_memory_space_constraint(base, pltpu.HBM))


def from_behind(block, distance):
    count = lax.axis_size("ta")
    return lax.ppermute(block, "ta", [(i - distance, i) for i in range(distance, count)])


def exchange(block):
    return lax.all_to_all(block, "ka", split_axis=0, concat_axis=0, tiled=True)


def on_device(green, energies, reach):
    table = tables(K)
    time = lax.axis_index("ka") * PART + lax.broadcasted_iota(jnp.int32, (PART, MEM), 0)
    lag = (time - lax.broadcasted_iota(jnp.int32, (PART, MEM), 1)) & (MEM - 1)
    mine = lax.dynamic_slice_in_dim(reach, lax.axis_index("ka") * PART, PART)
    keep = (lag < mine[:, None]).astype(F32)

    def inputs(own, low, chunk):
        spread = exchange(chunk)
        near, far = from_behind(own, 1), from_behind(low, 2)
        return exchange(self_energy(keep, table, spread)), own, low, near, far

    x, *rest = prepare(green)
    for last in (False, True):
        ahead, *rest = stage(True, False, energies, *inputs(*rest), x)
        x, *rest = stage(False, last, energies, *inputs(*rest), ahead)
    return x


def solution(mesh):
    in_specs = (P(None, "ka", "ta", None), P("ka"), P("ta"))
    out_specs = P(None, "ka", "ta", None)
    return jax.shard_map(
        on_device, mesh=mesh, in_specs=in_specs, out_specs=out_specs, check_vma=False
    )
```

```python
import jax
import jax.numpy as jnp
import numpy as np
from jax import lax
from jax.experimental import pallas as pl
from jax.experimental.pallas import tpu as pltpu
from jax.sharding import PartitionSpec as P


K = 256
MEM = 128
ROWS = 64
OWN = 16
GROUP = 16
PART = 4
PITCH = 17
KB = 8
STEPS = OWN // KB
PIECES = 4
MIB = 2**20

quadrature = 0.0625
step_size = 0.25

F32 = jnp.float32
BF16 = jnp.bfloat16


def tables(count):
    numbers = np.arange(count)
    phase = (numbers[:, None] * numbers[None, :] % count) * (2.0 * np.pi / count)
    both = np.concatenate([np.cos(phase), np.sin(phase)], 0) / np.sqrt(count)
    return jnp.asarray(both.astype(np.float32).astype(jnp.bfloat16))


def grids():
    row = lax.broadcasted_iota(jnp.int32, (ROWS, MEM), 0)
    lane = lax.broadcasted_iota(jnp.int32, (ROWS, MEM), 1)
    return row, lane


def turn_over(block):
    row, lane = grids()
    index = (row - lane) & (MEM - 1)
    pieces = [
        jnp.take_along_axis(block[i : i + 8], index[i : i + 8], axis=1) for i in range(0, ROWS, 8)
    ]
    return jnp.concatenate(pieces, 0)


def half_turn(block):
    return pltpu.roll(block, MEM // 2, 1)


def self_energy_kernel(keep, table, x, out, y, sems):
    def save(pair):
        here = pl.ds(2 * pair, 2)
        return pltpu.make_async_copy(y.at[:, :, here], out.at[:, :, here], sems.at[pair])

    cosines, sines = table[:K], table[K:]
    forward = jnp.concatenate(
        [
            jnp.concatenate([cosines, -sines], 1),
            jnp.concatenate([sines, cosines], 1),
        ],
        0,
    )
    inverse = jnp.concatenate(
        [
            jnp.concatenate([cosines, sines], 1),
            jnp.concatenate([-sines, cosines], 1),
        ],
        0,
    )
    for pair in range(2):
        rows = []
        for part in range(2):
            sides = [x[:, part, 2 * pair + i].reshape(K, MEM) for i in range(2)]
            rows.append(jnp.concatenate(sides, 1))
        field = jnp.dot(forward, jnp.concatenate(rows, 0), preferred_element_type=F32)
        re, im = field[:K], field[K:]
        weight = -(re * re + im * im)
        z = jnp.concatenate([(weight * re).astype(BF16), (weight * im).astype(BF16)], 0)
        both = jnp.dot(inverse, z, preferred_element_type=F32)
        sigma = both[:K], both[K:]
        for part in range(2):
            for i in range(2):
                side = sigma[part][:, i * MEM : (i + 1) * MEM]
                kept = keep[2 * pair + i : 2 * pair + i + 1, :] > 0
                side = jnp.where(kept, side, 0.0).astype(BF16)
                y[:, part, 2 * pair + i] = side.reshape(GROUP, OWN, MEM)
        save(pair).start()
    for pair in range(2):
        save(pair).wait()


CHUNK = (GROUP, 2, PART, OWN, MEM)
STATE = (2, OWN, ROWS, MEM)
FAR = (OWN, ROWS, MEM)
HBM = pl.BlockSpec(memory_space=pltpu.HBM)
SMEM = pl.BlockSpec(memory_space=pltpu.SMEM)
VMEM = pl.BlockSpec(memory_space=pltpu.VMEM)


def params(mib):
    return pltpu.CompilerParams(vmem_limit_bytes=int(mib * MIB))


def self_energy(keep, table, spread):
    return pl.pallas_call(
        self_energy_kernel,
        in_specs=[VMEM, VMEM, VMEM],
        out_specs=HBM,
        out_shape=pltpu.HBM(CHUNK, BF16),
        scratch_shapes=[pltpu.VMEM(CHUNK, BF16), pltpu.SemaphoreType.DMA((2,))],
        compiler_params=params(12),
        name="self_energy",
    )(keep, table, spread)


def piece(ref, q, size):
    here = pl.ds(q * size, size)
    return ref.at[here] if len(ref.shape) == 3 else ref.at[:, here]


def mover(pairs, sems, first, size=KB):
    def move(n, q):
        source, target = pairs[n]
        return pltpu.make_async_copy(piece(source, q, size), piece(target, q, size), sems.at[first + n, q])

    return move


def send_chunk(turned, block, chunk, sems):
    copies = []
    for first in range(0, GROUP, GROUP // PIECES):
        here = pl.ds(first, GROUP // PIECES)
        for d in range(first, first + GROUP // PIECES):
            for c in range(2):
                for j in range(PART):
                    t = (d * PART + j) * PITCH
                    block[d, c, j] = turned[c, t : t + OWN, :].astype(BF16)
        sem = sems.at[len(copies)]
        copies.append(pltpu.make_async_copy(block.at[here], chunk.at[here], sem))
        copies[-1].start()
    return copies


def emit(k, value, turned, near, far):
    row, lane = grids()
    causal = lane <= row
    low = []
    for c in range(2):
        turned[c, pl.ds(k, ROWS, stride=PITCH), :] = value[c]
        near[c, k] = value[c].astype(BF16)
        low.append(jnp.where(causal, value[c], 0.0))
    far[k] = (low[0] + half_turn(low[1])).astype(BF16)


def prepare_kernel(x_in, out, near, far, chunk, x, y, turned, block, sems, sem):
    load = mover([(x_in, x)], sems, 0, 4)
    pairs = [(y, out)]
    save = mover(pairs, sems, 1, 4)
    for q in range(OWN // 4):
        load(0, q).start()

    def step(q, carry):
        load(0, q).wait()
        for i in range(4):
            k = q * 4 + i
            value = [turn_over(x[c, k]) for c in range(2)]
            for c in range(2):
                y[c, k] = value[c]
            emit(k, value, turned, near, far)
        return carry

    lax.fori_loop(0, OWN // 4, step, 0)
    copies = send_chunk(turned, block, chunk, sem)
    for n in range(len(pairs)):
        for q in range(OWN // 4):
            save(n, q).start()
    for n in range(len(pairs)):
        for q in range(OWN // 4):
            save(n, q).wait()
    for copy in copies:
        copy.wait()


WIDE = pltpu.HBM(STATE, F32)
EMITTED = [pltpu.VMEM(STATE, BF16), pltpu.VMEM(FAR, BF16), pltpu.HBM(CHUNK, BF16)]


def emitting():
    return [
        pltpu.VMEM(STATE, BF16),
        pltpu.VMEM(FAR, BF16),
        pltpu.VMEM((2, ROWS * PITCH, MEM), F32),
        pltpu.VMEM(CHUNK, BF16),
    ]


def prepare(x):
    scratch = pltpu.VMEM(STATE, F32)
    return pl.pallas_call(
        prepare_kernel,
        in_specs=[HBM],
        out_specs=[HBM, VMEM, VMEM, HBM],
        out_shape=[WIDE] + EMITTED,
        scratch_shapes=[scratch, scratch]
        + emitting()[2:]
        + [pltpu.SemaphoreType.DMA((2, OWN // 4)), pltpu.SemaphoreType.DMA((PIECES,))],
        compiler_params=params(16),
        name="prepare",
    )(pltpu.with_memory_space_constraint(x, pltpu.HBM))


def stage_kernel(first, last, *refs):
    refs = list(refs)
    energies, sigma, own, own_low, near, far, base_in = refs[:7]
    if last:
        out, base, result, held, sems = refs[7:]
    else:
        out, mine, low, chunk, base, result, held, sems, turned, block, chunk_sem = refs[7:]

    loads = [(base_in, base)]
    saves = [(result, out)]
    load = mover(loads, sems, 0)
    save = mover(saves, sems, len(loads))
    for q in range(STEPS):
        for n in range(len(loads)):
            load(n, q).start()

    for d in range(GROUP):
        for c in range(2):
            for j in range(PART):
                t = d * PART + j
                held[c, t * PITCH : t * PITCH + OWN, :] = sigma[d, c, j].astype(F32)

    row, lane = grids()
    causal = lane <= row
    own_side = causal | (lane >= ROWS)
    seen = lane <= row + ROWS
    lower = lane < ROWS

    def only(kept, block):
        return jnp.where(kept, block, jnp.zeros_like(block))

    def step(q, carry):
        for i in range(KB):
            k = q * KB + i
            left = []
            for c in range(2):
                memory = held[c, pl.ds(k, ROWS, stride=PITCH), :]
                inner = jnp.where(own_side, memory, 0.0).astype(BF16)
                outer = jnp.where(own_side, 0.0, memory).astype(BF16)
                left.append(jnp.concatenate([inner, outer[:, :ROWS]], 1))
            left = jnp.concatenate(left, 0)
            packed = far[k]
            away = (packed, half_turn(packed))
            sides = []
            for c in range(2):
                rows = [
                    only(~causal, own[c, k]),
                    only(seen, half_turn(near[c, k])),
                    only(lower, away[c]),
                ]
                sides.append(jnp.concatenate(rows, 0))
            early = jnp.dot(left, jnp.concatenate(sides, 1), preferred_element_type=F32)
            late = jnp.dot(left[:, :ROWS], own_low[k], preferred_element_type=F32)
            collide = (
                jnp.where(
                    causal,
                    late[:ROWS] - half_turn(late[ROWS:]),
                    early[:ROWS, :MEM] - early[ROWS:, MEM:],
                ),
                jnp.where(
                    causal,
                    late[ROWS:] + half_turn(late[:ROWS]),
                    early[ROWS:, :MEM] + early[:ROWS, MEM:],
                ),
            )
            for c in range(2):
                result[c, k] = quadrature * collide[c]
        for n in range(len(loads)):
            load(n, q).wait()
        for i in range(KB):
            k = q * KB + i
            collide = result[0, k], result[1, k]
            half = 0.5 * step_size
            if first:
                energy = energies[k]
                xr, xi = base[0, k], base[1, k]
                fr = energy * xi + collide[1]
                fi = -(energy * xr + collide[0])
                value = (xr + step_size * fr, xi + step_size * fi)
                result[0, k] = xr + half * (fr + energy * value[1])
                result[1, k] = xi + half * (fi - energy * value[0])
            else:
                value = (base[0, k] + half * collide[1], base[1, k] - half * collide[0])
                for c in range(2):
                    result[c, k] = turn_over(value[c]) if last else value[c]
            if not last:
                emit(k, value, turned, mine, low)
        for n in range(len(saves)):
            save(n, q).start()
        return carry

    lax.fori_loop(0, STEPS, step, 0)
    if not last:
        for copy in send_chunk(turned, block, chunk, chunk_sem):
            copy.wait()
    for q in range(STEPS):
        for n in range(len(saves)):
            save(n, q).wait()


def stage(first, last, energies, sigma, own, own_low, near, far, base):
    state = pltpu.VMEM(STATE, F32)
    scratch = [state, state, pltpu.VMEM((2, ROWS * PITCH, MEM), F32)]
    scratch += [pltpu.SemaphoreType.DMA((2, STEPS))]
    out_shape, spaces = [WIDE], [HBM]
    if not last:
        out_shape += EMITTED
        spaces += [VMEM, VMEM, HBM]
        scratch += emitting()[2:] + [pltpu.SemaphoreType.DMA((PIECES,))]

    def kernel(*refs):
        stage_kernel(first, last, *refs)

    return pl.pallas_call(
        kernel,
        in_specs=[SMEM] + [VMEM] * 5 + [HBM],
        out_specs=spaces,
        out_shape=out_shape,
        scratch_shapes=scratch,
        compiler_params=params(16),
        name="stage",
    )(energies, sigma, own, own_low, near, far, pltpu.with_memory_space_constraint(base, pltpu.HBM))


def from_behind(block, distance):
    count = lax.axis_size("ta")
    return lax.ppermute(block, "ta", [(i - distance, i) for i in range(distance, count)])


def exchange(block):
    return lax.all_to_all(block, "ka", split_axis=0, concat_axis=0, tiled=True)


def on_device(green, energies, reach):
    table = tables(K)
    time = lax.axis_index("ka") * PART + lax.broadcasted_iota(jnp.int32, (PART, MEM), 0)
    lag = (time - lax.broadcasted_iota(jnp.int32, (PART, MEM), 1)) & (MEM - 1)
    mine = lax.dynamic_slice_in_dim(reach, lax.axis_index("ka") * PART, PART)
    keep = (lag < mine[:, None]).astype(F32)

    def inputs(own, low, chunk):
        spread = exchange(chunk)
        near = from_behind(own, 1)
        far = from_behind(low, 2)
        sigma = self_energy(keep, table, spread)
        sigma = exchange(sigma)
        return sigma, own, low, near, far

    x, *rest = prepare(green)
    for counter in range(2):
        ahead, *rest = stage(True, False, energies, *inputs(*rest), x)
        last = counter == 1
        x, *rest = stage(False, last, energies, *inputs(*rest), ahead)
    return x


def solution(mesh):
    in_specs = (P(None, "ka", "ta", None), P("ka"), P("ta"))
    out_specs = P(None, "ka", "ta", None)
    return jax.shard_map(
        on_device, mesh=mesh, in_specs=in_specs, out_specs=out_specs, check_vma=False
    )
```

```python
import jax
import jax.numpy as jnp
import numpy as np
from jax import lax
from jax.experimental import pallas as pl
from jax.experimental.pallas import tpu as pltpu
from jax.sharding import PartitionSpec as P


K = 256
MEM = 128
ROWS = 64
OWN = 16
GROUP = 16
PART = 4
PITCH = 17
KB = 8
STEPS = OWN // KB
MIB = 2**20

quadrature = 0.0625
step_size = 0.25

F32 = jnp.float32
BF16 = jnp.bfloat16


def tables(count):
    numbers = np.arange(count)
    phase = (numbers[:, None] * numbers[None, :] % count) * (2.0 * np.pi / count)
    both = np.concatenate([np.cos(phase), np.sin(phase)], 0) / np.sqrt(count)
    return jnp.asarray(both.astype(np.float32).astype(jnp.bfloat16))


def grids():
    row = lax.broadcasted_iota(jnp.int32, (ROWS, MEM), 0)
    lane = lax.broadcasted_iota(jnp.int32, (ROWS, MEM), 1)
    return row, lane


def turn_over(block):
    row, lane = grids()
    index = (row - lane) & (MEM - 1)
    pieces = [
        jnp.take_along_axis(block[i : i + 8], index[i : i + 8], axis=1) for i in range(0, ROWS, 8)
    ]
    return jnp.concatenate(pieces, 0)


def half_turn(block):
    return pltpu.roll(block, MEM // 2, 1)


def self_energy_kernel(keep, table, x, out, y, sems):
    def save(pair):
        here = pl.ds(2 * pair, 2)
        return pltpu.make_async_copy(y.at[:, :, here], out.at[:, :, here], sems.at[pair])

    cosines, sines = table[:K], table[K:]
    forward = jnp.concatenate(
        [
            jnp.concatenate([cosines, -sines], 1),
            jnp.concatenate([sines, cosines], 1),
        ],
        0,
    )
    inverse = jnp.concatenate(
        [
            jnp.concatenate([cosines, sines], 1),
            jnp.concatenate([-sines, cosines], 1),
        ],
        0,
    )
    for pair in range(2):
        rows = []
        for part in range(2):
            sides = [x[:, part, 2 * pair + i].reshape(K, MEM) for i in range(2)]
            rows.append(jnp.concatenate(sides, 1))
        field = jnp.dot(forward, jnp.concatenate(rows, 0), preferred_element_type=F32)
        re, im = field[:K], field[K:]
        weight = -(re * re + im * im)
        z = jnp.concatenate([(weight * re).astype(BF16), (weight * im).astype(BF16)], 0)
        both = jnp.dot(inverse, z, preferred_element_type=F32)
        sigma = both[:K], both[K:]
        for part in range(2):
            for i in range(2):
                side = sigma[part][:, i * MEM : (i + 1) * MEM]
                kept = keep[2 * pair + i : 2 * pair + i + 1, :] > 0
                side = jnp.where(kept, side, 0.0).astype(BF16)
                y[:, part, 2 * pair + i] = side.reshape(GROUP, OWN, MEM)
        save(pair).start()
    for pair in range(2):
        save(pair).wait()


CHUNK = (GROUP, 2, PART, OWN, MEM)
STATE = (2, OWN, ROWS, MEM)
FAR = (OWN, ROWS, MEM)
HBM = pl.BlockSpec(memory_space=pltpu.HBM)
SMEM = pl.BlockSpec(memory_space=pltpu.SMEM)
VMEM = pl.BlockSpec(memory_space=pltpu.VMEM)


def params(mib):
    return pltpu.CompilerParams(vmem_limit_bytes=int(mib * MIB))


def self_energy(keep, table, spread):
    return pl.pallas_call(
        self_energy_kernel,
        in_specs=[VMEM, VMEM, VMEM],
        out_specs=HBM,
        out_shape=pltpu.HBM(CHUNK, BF16),
        scratch_shapes=[pltpu.VMEM(CHUNK, BF16), pltpu.SemaphoreType.DMA((2,))],
        compiler_params=params(12),
        name="self_energy",
    )(keep, table, spread)


def piece(ref, q, size):
    here = pl.ds(q * size, size)
    return ref.at[here] if len(ref.shape) == 3 else ref.at[:, here]


def mover(pairs, sems, first, size=KB):
    def move(n, q):
        source, target = pairs[n]
        return pltpu.make_async_copy(piece(source, q, size), piece(target, q, size), sems.at[first + n, q])

    return move


def chunk_copy(block, chunk, sems, q):
    here = pl.ds(q * (GROUP // STEPS), GROUP // STEPS)
    return pltpu.make_async_copy(block.at[here], chunk.at[here], sems.at[q])


def pack_chunk(turned, block, q):
    for d in range(q * (GROUP // STEPS), (q + 1) * (GROUP // STEPS)):
        for c in range(2):
            for j in range(PART):
                t = (d * PART + j) * PITCH
                block[d, c, j] = turned[c, t : t + OWN, :].astype(BF16)


def emit(turned, near, far):
    row, lane = grids()
    causal = lane <= row

    def step(q, carry):
        for i in range(4):
            k = q * 4 + i
            low = []
            for c in range(2):
                value = turned[c, pl.ds(k, ROWS, stride=PITCH), :]
                near[c, k] = value.astype(BF16)
                low.append(jnp.where(causal, value, 0.0))
            far[k] = (low[0] + half_turn(low[1])).astype(BF16)
        return carry

    lax.fori_loop(0, OWN // 4, step, 0)


def prepare_kernel(x_in, out, near, far, chunk, x, y, turned, block, sems, sem):
    load = mover([(x_in, x)], sems, 0)
    save = mover([(y, out)], sems, 1)
    for q in range(STEPS):
        load(0, q).start()

    def step(q, carry):
        load(0, q).wait()
        for i in range(KB):
            k = q * KB + i
            for c in range(2):
                value = turn_over(x[c, k])
                y[c, k] = value
                turned[c, pl.ds(k, ROWS, stride=PITCH), :] = value
        return carry

    lax.fori_loop(0, STEPS, step, 0)
    for q in range(STEPS):
        pack_chunk(turned, block, q)
        chunk_copy(block, chunk, sem, q).start()
    for q in range(STEPS):
        save(0, q).start()
    emit(turned, near, far)
    for q in range(STEPS):
        chunk_copy(block, chunk, sem, q).wait()
        save(0, q).wait()


WIDE = pltpu.HBM(STATE, F32)
EMITTED = [pltpu.VMEM(STATE, BF16), pltpu.VMEM(FAR, BF16), pltpu.HBM(CHUNK, BF16)]


def emitting():
    return [
        pltpu.VMEM(STATE, BF16),
        pltpu.VMEM(FAR, BF16),
        pltpu.VMEM((2, (ROWS + 1) * PITCH, MEM), F32),
        pltpu.VMEM(CHUNK, BF16),
    ]


def prepare(x):
    scratch = pltpu.VMEM(STATE, F32)
    return pl.pallas_call(
        prepare_kernel,
        in_specs=[HBM],
        out_specs=[HBM, VMEM, VMEM, HBM],
        out_shape=[WIDE] + EMITTED,
        scratch_shapes=[scratch, scratch]
        + emitting()[2:]
        + [pltpu.SemaphoreType.DMA((2, STEPS)), pltpu.SemaphoreType.DMA((STEPS,))],
        compiler_params=params(16),
        name="prepare",
    )(pltpu.with_memory_space_constraint(x, pltpu.HBM))


def stage_kernel(first, last, *refs):
    refs = list(refs)
    energies, sigma, own, own_low, near, far, base_in = refs[:7]
    if last:
        out, base, result, held, sems = refs[7:]
    else:
        out, mine, low, chunk, base, result, held, sems, turned, block, chunk_sem = refs[7:]

    loads = [(base_in, base)]
    saves = [(result, out)]
    load = mover(loads, sems, 0)
    save = mover(saves, sems, len(loads))
    for q in range(STEPS):
        for n in range(len(loads)):
            load(n, q).start()

    for d in range(GROUP):
        for c in range(2):
            for j in range(PART):
                t = d * PART + j
                held[c, t * PITCH : t * PITCH + OWN, :] = sigma[d, c, j].astype(F32)

    row, lane = grids()
    causal = lane <= row
    own_side = causal | (lane >= ROWS)
    seen = lane <= row + ROWS
    lower = lane < ROWS

    def only(kept, block):
        return jnp.where(kept, block, jnp.zeros_like(block))

    def step(q, carry):
        for i in range(KB):
            k = q * KB + i
            left = []
            for c in range(2):
                memory = held[c, pl.ds(k, ROWS, stride=PITCH), :]
                inner = jnp.where(own_side, memory, 0.0).astype(BF16)
                outer = jnp.where(own_side, 0.0, memory).astype(BF16)
                left.append(jnp.concatenate([inner, outer[:, :ROWS]], 1))
            left = jnp.concatenate(left, 0)
            packed = far[k]
            away = (packed, half_turn(packed))
            sides = []
            for c in range(2):
                rows = [
                    only(~causal, own[c, k]),
                    only(seen, half_turn(near[c, k])),
                    only(lower, away[c]),
                ]
                sides.append(jnp.concatenate(rows, 0))
            early = jnp.dot(left, jnp.concatenate(sides, 1), preferred_element_type=F32)
            late = jnp.dot(left[:, :ROWS], own_low[k], preferred_element_type=F32)
            collide = (
                jnp.where(
                    causal,
                    late[:ROWS] - half_turn(late[ROWS:]),
                    early[:ROWS, :MEM] - early[ROWS:, MEM:],
                ),
                jnp.where(
                    causal,
                    late[ROWS:] + half_turn(late[:ROWS]),
                    early[ROWS:, :MEM] + early[:ROWS, MEM:],
                ),
            )
            for c in range(2):
                result[c, k] = quadrature * collide[c]
        return carry

    def advance(q, carry):
        for n in range(len(loads)):
            load(n, q).wait()
        for i in range(KB):
            k = q * KB + i
            collide = result[0, k], result[1, k]
            half = 0.5 * step_size
            if first:
                energy = energies[k]
                xr, xi = base[0, k], base[1, k]
                fr = energy * xi + collide[1]
                fi = -(energy * xr + collide[0])
                value = (xr + step_size * fr, xi + step_size * fi)
                result[0, k] = xr + half * (fr + energy * value[1])
                result[1, k] = xi + half * (fi - energy * value[0])
            else:
                value = (base[0, k] + half * collide[1], base[1, k] - half * collide[0])
                for c in range(2):
                    result[c, k] = turn_over(value[c]) if last else value[c]
            if not last:
                for c in range(2):
                    turned[c, pl.ds(k, ROWS, stride=PITCH), :] = value[c]
        for n in range(len(saves)):
            save(n, q).start()
        return carry

    lax.fori_loop(0, STEPS, step, 0)
    lax.fori_loop(0, STEPS, advance, 0)
    if not last:
        for q in range(STEPS):
            pack_chunk(turned, block, q)
            chunk_copy(block, chunk, chunk_sem, q).start()
        emit(turned, mine, low)
        for q in range(STEPS):
            chunk_copy(block, chunk, chunk_sem, q).wait()
    for q in range(STEPS):
        for n in range(len(saves)):
            save(n, q).wait()


def stage(first, last, energies, sigma, own, own_low, near, far, base):
    state = pltpu.VMEM(STATE, F32)
    scratch = [state, state, pltpu.VMEM((2, (ROWS + 1) * PITCH, MEM), F32)]
    scratch += [pltpu.SemaphoreType.DMA((2, STEPS))]
    out_shape, spaces = [WIDE], [HBM]
    if not last:
        out_shape += EMITTED
        spaces += [VMEM, VMEM, HBM]
        scratch += emitting()[2:] + [pltpu.SemaphoreType.DMA((STEPS,))]

    def kernel(*refs):
        stage_kernel(first, last, *refs)

    return pl.pallas_call(
        kernel,
        in_specs=[SMEM] + [VMEM] * 5 + [HBM],
        out_specs=spaces,
        out_shape=out_shape,
        scratch_shapes=scratch,
        compiler_params=params(16),
        name="stage",
    )(energies, sigma, own, own_low, near, far, pltpu.with_memory_space_constraint(base, pltpu.HBM))


def from_behind(block, distance):
    count = lax.axis_size("ta")
    return lax.ppermute(block, "ta", [(i - distance, i) for i in range(distance, count)])


def exchange(block):
    return lax.all_to_all(block, "ka", split_axis=0, concat_axis=0, tiled=True)


def on_device(green, energies, reach):
    table = tables(K)
    time = lax.axis_index("ka") * PART + lax.broadcasted_iota(jnp.int32, (PART, MEM), 0)
    lag = (time - lax.broadcasted_iota(jnp.int32, (PART, MEM), 1)) & (MEM - 1)
    mine = lax.dynamic_slice_in_dim(reach, lax.axis_index("ka") * PART, PART)
    keep = (lag < mine[:, None]).astype(F32)

    def inputs(own, low, chunk):
        spread = exchange(chunk)
        near = from_behind(own, 1)
        far = from_behind(low, 2)
        sigma = self_energy(keep, table, spread)
        sigma = exchange(sigma)
        return sigma, own, low, near, far

    x, *rest = prepare(green)
    for counter in range(2):
        ahead, *rest = stage(True, False, energies, *inputs(*rest), x)
        last = counter == 1
        x, *rest = stage(False, last, energies, *inputs(*rest), ahead)
    return x


def solution(mesh):
    in_specs = (P(None, "ka", "ta", None), P("ka"), P("ta"))
    out_specs = P(None, "ka", "ta", None)
    return jax.shard_map(
        on_device, mesh=mesh, in_specs=in_specs, out_specs=out_specs, check_vma=False
    )
```

```python
import jax
import jax.numpy as jnp
import numpy as np
from jax import lax
from jax.experimental import pallas as pl
from jax.experimental.pallas import tpu as pltpu
from jax.sharding import PartitionSpec as P


K = 256
MEM = 128
ROWS = 64
OWN = 16
GROUP = 16
PART = 4
PITCH = 17
KB = 8
STEPS = OWN // KB
MIB = 2**20

quadrature = 0.0625
step_size = 0.25

F32 = jnp.float32
BF16 = jnp.bfloat16


def tables(count):
    numbers = np.arange(count)
    phase = (numbers[:, None] * numbers[None, :] % count) * (2.0 * np.pi / count)
    both = np.concatenate([np.cos(phase), np.sin(phase)], 0) / np.sqrt(count)
    return jnp.asarray(both.astype(np.float32).astype(jnp.bfloat16))


def grids():
    row = lax.broadcasted_iota(jnp.int32, (ROWS, MEM), 0)
    lane = lax.broadcasted_iota(jnp.int32, (ROWS, MEM), 1)
    return row, lane


def turn_over(block):
    row, lane = grids()
    index = (row - lane) & (MEM - 1)
    pieces = [
        jnp.take_along_axis(block[i : i + 8], index[i : i + 8], axis=1) for i in range(0, ROWS, 8)
    ]
    return jnp.concatenate(pieces, 0)


def half_turn(block):
    return pltpu.roll(block, MEM // 2, 1)


def self_energy_kernel(keep, table, x, out, y, sems):
    def save(pair):
        here = pl.ds(2 * pair, 2)
        return pltpu.make_async_copy(y.at[:, :, here], out.at[:, :, here], sems.at[pair])

    cosines, sines = table[:K], table[K:]
    forward = jnp.concatenate(
        [
            jnp.concatenate([cosines, -sines], 1),
            jnp.concatenate([sines, cosines], 1),
        ],
        0,
    )
    inverse = jnp.concatenate(
        [
            jnp.concatenate([cosines, sines], 1),
            jnp.concatenate([-sines, cosines], 1),
        ],
        0,
    )
    for pair in range(2):
        rows = []
        for part in range(2):
            sides = [x[:, part, 2 * pair + i].reshape(K, MEM) for i in range(2)]
            rows.append(jnp.concatenate(sides, 1))
        field = jnp.dot(forward, jnp.concatenate(rows, 0), preferred_element_type=F32)
        re, im = field[:K], field[K:]
        weight = -(re * re + im * im)
        z = jnp.concatenate([(weight * re).astype(BF16), (weight * im).astype(BF16)], 0)
        both = jnp.dot(inverse, z, preferred_element_type=F32)
        sigma = both[:K], both[K:]
        for part in range(2):
            for i in range(2):
                side = sigma[part][:, i * MEM : (i + 1) * MEM]
                kept = keep[2 * pair + i : 2 * pair + i + 1, :] > 0
                side = jnp.where(kept, side, 0.0).astype(BF16)
                y[:, part, 2 * pair + i] = side.reshape(GROUP, OWN, MEM)
        save(pair).start()
    for pair in range(2):
        save(pair).wait()


CHUNK = (GROUP, 2, PART, OWN, MEM)
STATE = (2, OWN, ROWS, MEM)
FAR = (OWN, ROWS, MEM)
HBM = pl.BlockSpec(memory_space=pltpu.HBM)
VMEM = pl.BlockSpec(memory_space=pltpu.VMEM)


def params(mib):
    return pltpu.CompilerParams(vmem_limit_bytes=int(mib * MIB))


def self_energy(keep, table, spread):
    return pl.pallas_call(
        self_energy_kernel,
        in_specs=[VMEM, VMEM, VMEM],
        out_specs=HBM,
        out_shape=pltpu.HBM(CHUNK, BF16),
        scratch_shapes=[pltpu.VMEM(CHUNK, BF16), pltpu.SemaphoreType.DMA((2,))],
        compiler_params=params(12),
        name="self_energy",
    )(keep, table, spread)


def piece(ref, q, size):
    here = pl.ds(q * size, size)
    return ref.at[here] if len(ref.shape) == 3 else ref.at[:, here]


def mover(pairs, sems, first, size=KB):
    def move(n, q):
        source, target = pairs[n]
        return pltpu.make_async_copy(piece(source, q, size), piece(target, q, size), sems.at[first + n, q])

    return move


def chunk_copy(block, chunk, sems, q):
    here = pl.ds(q * (GROUP // STEPS), GROUP // STEPS)
    return pltpu.make_async_copy(block.at[here], chunk.at[here], sems.at[q])


def pack_chunk(turned, block, q):
    for d in range(q * (GROUP // STEPS), (q + 1) * (GROUP // STEPS)):
        for c in range(2):
            for j in range(PART):
                t = (d * PART + j) * PITCH
                block[d, c, j] = turned[c, t : t + OWN, :].astype(BF16)


def emit(turned, near, far):
    row, lane = grids()
    causal = lane <= row

    def step(q, carry):
        for i in range(4):
            k = q * 4 + i
            low = []
            for c in range(2):
                value = turned[c, pl.ds(k, ROWS, stride=PITCH), :]
                near[c, k] = value.astype(BF16)
                low.append(jnp.where(causal, value, 0.0))
            far[k] = (low[0] + half_turn(low[1])).astype(BF16)
        return carry

    lax.fori_loop(0, OWN // 4, step, 0)


def prepare_kernel(x_in, out, near, far, chunk, x, y, turned, block, sems, sem):
    load = mover([(x_in, x)], sems, 0)
    save = mover([(y, out)], sems, 1)
    for q in range(STEPS):
        load(0, q).start()

    def step(q, carry):
        load(0, q).wait()
        for i in range(KB):
            k = q * KB + i
            for c in range(2):
                value = turn_over(x[c, k])
                y[c, k] = value
                turned[c, pl.ds(k, ROWS, stride=PITCH), :] = value
        return carry

    lax.fori_loop(0, STEPS, step, 0)
    for q in range(STEPS):
        pack_chunk(turned, block, q)
        chunk_copy(block, chunk, sem, q).start()
    for q in range(STEPS):
        save(0, q).start()
    emit(turned, near, far)
    for q in range(STEPS):
        chunk_copy(block, chunk, sem, q).wait()
        save(0, q).wait()


WIDE = pltpu.HBM(STATE, F32)
EMITTED = [pltpu.VMEM(STATE, BF16), pltpu.VMEM(FAR, BF16), pltpu.HBM(CHUNK, BF16)]


def emitting():
    return [
        pltpu.VMEM(STATE, BF16),
        pltpu.VMEM(FAR, BF16),
        pltpu.VMEM((2, (ROWS + 1) * PITCH, MEM), F32),
        pltpu.VMEM(CHUNK, BF16),
    ]


def prepare(x):
    scratch = pltpu.VMEM(STATE, F32)
    return pl.pallas_call(
        prepare_kernel,
        in_specs=[HBM],
        out_specs=[HBM, VMEM, VMEM, HBM],
        out_shape=[WIDE] + EMITTED,
        scratch_shapes=[scratch, scratch]
        + emitting()[2:]
        + [pltpu.SemaphoreType.DMA((2, STEPS)), pltpu.SemaphoreType.DMA((STEPS,))],
        compiler_params=params(16),
        name="prepare",
    )(pltpu.with_memory_space_constraint(x, pltpu.HBM))


def stage_kernel(first, last, *refs):
    refs = list(refs)
    sigma, own, own_low, near, far, base_in = refs[:6]
    refs = refs[6:]
    energies = refs.pop(0) if first else None
    if last:
        out, base, result, held, sems = refs
    else:
        out, mine, low, chunk, base, result, held, sems, turned, block, chunk_sem = refs

    loads = [(base_in, base)]
    saves = [(result, out)]
    load = mover(loads, sems, 0)
    save = mover(saves, sems, len(loads))
    for q in range(STEPS):
        for n in range(len(loads)):
            load(n, q).start()

    for d in range(GROUP):
        for c in range(2):
            for j in range(PART):
                t = d * PART + j
                held[c, t * PITCH : t * PITCH + OWN, :] = sigma[d, c, j].astype(F32)

    row, lane = grids()
    causal = lane <= row
    own_side = causal | (lane >= ROWS)
    seen = lane <= row + ROWS
    lower = lane < ROWS

    def only(kept, block):
        return jnp.where(kept, block, jnp.zeros_like(block))

    def step(q, carry):
        for i in range(KB):
            k = q * KB + i
            left = []
            for c in range(2):
                memory = held[c, pl.ds(k, ROWS, stride=PITCH), :]
                inner = jnp.where(own_side, memory, 0.0).astype(BF16)
                outer = jnp.where(own_side, 0.0, memory).astype(BF16)
                left.append(jnp.concatenate([inner, outer[:, :ROWS]], 1))
            left = jnp.concatenate(left, 0)
            packed = far[k]
            away = (packed, half_turn(packed))
            sides = []
            for c in range(2):
                rows = [
                    only(~causal, own[c, k]),
                    only(seen, half_turn(near[c, k])),
                    only(lower, away[c]),
                ]
                sides.append(jnp.concatenate(rows, 0))
            early = jnp.dot(left, jnp.concatenate(sides, 1), preferred_element_type=F32)
            late = jnp.dot(left[:, :ROWS], own_low[k], preferred_element_type=F32)
            collide = (
                jnp.where(
                    causal,
                    late[:ROWS] - half_turn(late[ROWS:]),
                    early[:ROWS, :MEM] - early[ROWS:, MEM:],
                ),
                jnp.where(
                    causal,
                    late[ROWS:] + half_turn(late[:ROWS]),
                    early[ROWS:, :MEM] + early[:ROWS, MEM:],
                ),
            )
            for c in range(2):
                result[c, k] = quadrature * collide[c]
        return carry

    def advance(q, carry):
        for n in range(len(loads)):
            load(n, q).wait()
        for i in range(KB):
            k = q * KB + i
            collide = result[0, k], result[1, k]
            half = 0.5 * step_size
            if first:
                energy = energies[pl.ds(k, 1), :]
                xr, xi = base[0, k], base[1, k]
                fr = energy * xi + collide[1]
                fi = -(energy * xr + collide[0])
                value = (xr + step_size * fr, xi + step_size * fi)
                result[0, k] = xr + half * (fr + energy * value[1])
                result[1, k] = xi + half * (fi - energy * value[0])
            else:
                value = (base[0, k] + half * collide[1], base[1, k] - half * collide[0])
                for c in range(2):
                    result[c, k] = turn_over(value[c]) if last else value[c]
            if not last:
                for c in range(2):
                    turned[c, pl.ds(k, ROWS, stride=PITCH), :] = value[c]
        for n in range(len(saves)):
            save(n, q).start()
        return carry

    lax.fori_loop(0, STEPS, step, 0)
    lax.fori_loop(0, STEPS, advance, 0)
    if not last:
        for q in range(STEPS):
            pack_chunk(turned, block, q)
            chunk_copy(block, chunk, chunk_sem, q).start()
        emit(turned, mine, low)
        for q in range(STEPS):
            chunk_copy(block, chunk, chunk_sem, q).wait()
    for q in range(STEPS):
        for n in range(len(saves)):
            save(n, q).wait()


def stage(first, last, energies, sigma, own, own_low, near, far, base):
    state = pltpu.VMEM(STATE, F32)
    scratch = [state, state, pltpu.VMEM((2, (ROWS + 1) * PITCH, MEM), F32)]
    scratch += [pltpu.SemaphoreType.DMA((2, STEPS))]
    out_shape, spaces = [WIDE], [HBM]
    if not last:
        out_shape += EMITTED
        spaces += [VMEM, VMEM, HBM]
        scratch += emitting()[2:] + [pltpu.SemaphoreType.DMA((STEPS,))]

    def kernel(*refs):
        stage_kernel(first, last, *refs)

    operands = [sigma, own, own_low, near, far, pltpu.with_memory_space_constraint(base, pltpu.HBM)]
    in_specs = [VMEM] * 5 + [HBM]
    if first:
        operands.append(energies)
        in_specs.append(VMEM)
    return pl.pallas_call(
        kernel,
        in_specs=in_specs,
        out_specs=spaces,
        out_shape=out_shape,
        scratch_shapes=scratch,
        compiler_params=params(16),
        name="stage",
    )(*operands)


def from_behind(block, distance):
    count = lax.axis_size("ta")
    return lax.ppermute(block, "ta", [(i - distance, i) for i in range(distance, count)])


def exchange(block):
    return lax.all_to_all(block, "ka", split_axis=0, concat_axis=0, tiled=True)


def on_device(green, energies, reach):
    table = tables(K)
    time = lax.axis_index("ka") * PART + lax.broadcasted_iota(jnp.int32, (PART, MEM), 0)
    lag = (time - lax.broadcasted_iota(jnp.int32, (PART, MEM), 1)) & (MEM - 1)
    mine = lax.dynamic_slice_in_dim(reach, lax.axis_index("ka") * PART, PART)
    keep = (lag < mine[:, None]).astype(F32)

    energies = jnp.broadcast_to(energies[:, None], (OWN, MEM))

    def inputs(own, low, chunk):
        spread = exchange(chunk)
        near = from_behind(own, 1)
        far = from_behind(low, 2)
        sigma = self_energy(keep, table, spread)
        sigma = exchange(sigma)
        return sigma, own, low, near, far

    x, *rest = prepare(green)
    for counter in range(2):
        ahead, *rest = stage(True, False, energies, *inputs(*rest), x)
        last = counter == 1
        x, *rest = stage(False, last, energies, *inputs(*rest), ahead)
    return x


def solution(mesh):
    in_specs = (P(None, "ka", "ta", None), P("ka"), P("ta"))
    out_specs = P(None, "ka", "ta", None)
    return jax.shard_map(
        on_device, mesh=mesh, in_specs=in_specs, out_specs=out_specs, check_vma=False
    )
```

```python
import jax
import jax.numpy as jnp
import numpy as np
from jax import lax
from jax.experimental import pallas as pl
from jax.experimental.pallas import tpu as pltpu
from jax.sharding import PartitionSpec as P


K = 256
MEM = 128
ROWS = 64
OWN = 16
GROUP = 16
PART = 4
PITCH = 17
KB = 8
STEPS = OWN // KB
MIB = 2**20

quadrature = 0.0625
step_size = 0.25

F32 = jnp.float32
BF16 = jnp.bfloat16


def tables(count):
    numbers = np.arange(count)
    phase = (numbers[:, None] * numbers[None, :] % count) * (2.0 * np.pi / count)
    both = np.concatenate([np.cos(phase), np.sin(phase)], 0) / np.sqrt(count)
    return jnp.asarray(both.astype(np.float32).astype(jnp.bfloat16))


def grids():
    row = lax.broadcasted_iota(jnp.int32, (ROWS, MEM), 0)
    lane = lax.broadcasted_iota(jnp.int32, (ROWS, MEM), 1)
    return row, lane


def turn_over(block):
    row, lane = grids()
    index = (row - lane) & (MEM - 1)
    pieces = [
        jnp.take_along_axis(block[i : i + 8], index[i : i + 8], axis=1) for i in range(0, ROWS, 8)
    ]
    return jnp.concatenate(pieces, 0)


def half_turn(block):
    return pltpu.roll(block, MEM // 2, 1)


def self_energy_kernel(keep, table, x, out, y, sems):
    def save(pair):
        here = pl.ds(2 * pair, 2)
        return pltpu.make_async_copy(y.at[:, :, here], out.at[:, :, here], sems.at[pair])

    cosines, sines = table[:K], table[K:]
    forward = jnp.concatenate(
        [
            jnp.concatenate([cosines, -sines], 1),
            jnp.concatenate([sines, cosines], 1),
        ],
        0,
    )
    inverse = jnp.concatenate(
        [
            jnp.concatenate([cosines, sines], 1),
            jnp.concatenate([-sines, cosines], 1),
        ],
        0,
    )
    for pair in range(2):
        rows = []
        for part in range(2):
            sides = [x[:, part, 2 * pair + i].reshape(K, MEM) for i in range(2)]
            rows.append(jnp.concatenate(sides, 1))
        field = jnp.dot(forward, jnp.concatenate(rows, 0), preferred_element_type=F32)
        re, im = field[:K], field[K:]
        weight = -(re * re + im * im)
        z = jnp.concatenate([(weight * re).astype(BF16), (weight * im).astype(BF16)], 0)
        both = jnp.dot(inverse, z, preferred_element_type=F32)
        sigma = both[:K], both[K:]
        for part in range(2):
            for i in range(2):
                side = sigma[part][:, i * MEM : (i + 1) * MEM]
                kept = keep[2 * pair + i : 2 * pair + i + 1, :] > 0
                side = jnp.where(kept, side, 0.0).astype(BF16)
                y[:, part, 2 * pair + i] = side.reshape(GROUP, OWN, MEM)
        save(pair).start()
    for pair in range(2):
        save(pair).wait()


CHUNK = (GROUP, 2, PART, OWN, MEM)
STATE = (2, OWN, ROWS, MEM)
FAR = (OWN, ROWS, MEM)
HBM = pl.BlockSpec(memory_space=pltpu.HBM)
VMEM = pl.BlockSpec(memory_space=pltpu.VMEM)


def params(mib):
    return pltpu.CompilerParams(vmem_limit_bytes=int(mib * MIB))


def self_energy(keep, table, spread):
    return pl.pallas_call(
        self_energy_kernel,
        in_specs=[VMEM, VMEM, VMEM],
        out_specs=HBM,
        out_shape=pltpu.HBM(CHUNK, BF16),
        scratch_shapes=[pltpu.VMEM(CHUNK, BF16), pltpu.SemaphoreType.DMA((2,))],
        compiler_params=params(12),
        name="self_energy",
    )(keep, table, spread)


def piece(ref, q, size):
    here = pl.ds(q * size, size)
    return ref.at[here] if len(ref.shape) == 3 else ref.at[:, here]


def mover(pairs, sems, first, size=KB):
    def move(n, q):
        source, target = pairs[n]
        return pltpu.make_async_copy(piece(source, q, size), piece(target, q, size), sems.at[first + n, q])

    return move


def chunk_copy(block, chunk, sems, q):
    here = pl.ds(q * (GROUP // STEPS), GROUP // STEPS)
    return pltpu.make_async_copy(block.at[here], chunk.at[here], sems.at[q])


def pack_chunk(turned, block, q):
    for d in range(q * (GROUP // STEPS), (q + 1) * (GROUP // STEPS)):
        for c in range(2):
            for j in range(PART):
                t = (d * PART + j) * PITCH
                block[d, c, j] = turned[c, t : t + OWN, :].astype(BF16)


def emit(turned, near, far):
    row, lane = grids()
    causal = lane <= row

    def step(q, carry):
        for i in range(4):
            k = q * 4 + i
            low = []
            for c in range(2):
                value = turned[c, pl.ds(k, ROWS, stride=PITCH), :]
                near[c, k] = value.astype(BF16)
                low.append(jnp.where(causal, value, 0.0))
            far[k] = (low[0] + half_turn(low[1])).astype(BF16)
        return carry

    lax.fori_loop(0, OWN // 4, step, 0)


def prepare_kernel(x_in, out, near, far, chunk, x, y, turned, block, sems, sem):
    load = mover([(x_in, x)], sems, 0)
    save = mover([(y, out)], sems, 1)
    for q in range(STEPS):
        load(0, q).start()

    def step(q, carry):
        load(0, q).wait()
        for i in range(KB):
            k = q * KB + i
            for c in range(2):
                value = turn_over(x[c, k])
                y[c, k] = value
                turned[c, pl.ds(k, ROWS, stride=PITCH), :] = value
        save(0, q).start()
        return carry

    lax.fori_loop(0, STEPS, step, 0)
    for q in range(STEPS):
        pack_chunk(turned, block, q)
        chunk_copy(block, chunk, sem, q).start()
    emit(turned, near, far)
    for q in range(STEPS):
        chunk_copy(block, chunk, sem, q).wait()
        save(0, q).wait()


WIDE = pltpu.HBM(STATE, F32)
EMITTED = [pltpu.VMEM(STATE, BF16), pltpu.VMEM(FAR, BF16), pltpu.HBM(CHUNK, BF16)]


def emitting():
    return [
        pltpu.VMEM(STATE, BF16),
        pltpu.VMEM(FAR, BF16),
        pltpu.VMEM((2, (ROWS + 1) * PITCH, MEM), F32),
        pltpu.VMEM(CHUNK, BF16),
    ]


def prepare(x):
    scratch = pltpu.VMEM(STATE, F32)
    return pl.pallas_call(
        prepare_kernel,
        in_specs=[HBM],
        out_specs=[HBM, VMEM, VMEM, HBM],
        out_shape=[WIDE] + EMITTED,
        scratch_shapes=[scratch, scratch]
        + emitting()[2:]
        + [pltpu.SemaphoreType.DMA((2, STEPS)), pltpu.SemaphoreType.DMA((STEPS,))],
        compiler_params=params(16),
        name="prepare",
    )(pltpu.with_memory_space_constraint(x, pltpu.HBM))


def stage_kernel(first, last, *refs):
    refs = list(refs)
    sigma, own, own_low, near, far, base_in = refs[:6]
    refs = refs[6:]
    energies = refs.pop(0) if first else None
    if last:
        out, base, result, held, sems = refs
    else:
        out, mine, low, chunk, base, result, held, sems, turned, block, chunk_sem = refs

    loads = [(base_in, base)]
    saves = [(result, out)]
    load = mover(loads, sems, 0)
    save = mover(saves, sems, len(loads))
    for q in range(STEPS):
        for n in range(len(loads)):
            load(n, q).start()

    for d in range(GROUP):
        for c in range(2):
            for j in range(PART):
                t = d * PART + j
                held[c, t * PITCH : t * PITCH + OWN, :] = sigma[d, c, j].astype(F32)

    row, lane = grids()
    causal = lane <= row
    own_side = causal | (lane >= ROWS)
    seen = lane <= row + ROWS
    lower = lane < ROWS

    def only(kept, block):
        return jnp.where(kept, block, jnp.zeros_like(block))

    def step(q, carry):
        for i in range(KB):
            k = q * KB + i
            left = []
            for c in range(2):
                memory = held[c, pl.ds(k, ROWS, stride=PITCH), :].astype(BF16)
                inner = only(own_side, memory)
                outer = only(~own_side, memory)
                left.append(jnp.concatenate([inner, outer[:, :ROWS]], 1))
            left = jnp.concatenate(left, 0)
            packed = far[k]
            away = (packed, half_turn(packed))
            sides = []
            for c in range(2):
                rows = [
                    only(~causal, own[c, k]),
                    only(seen, half_turn(near[c, k])),
                    only(lower, away[c]),
                ]
                sides.append(jnp.concatenate(rows, 0))
            early = jnp.dot(left, jnp.concatenate(sides, 1), preferred_element_type=F32)
            late = jnp.dot(left[:, :ROWS], own_low[k], preferred_element_type=F32)
            collide = (
                jnp.where(
                    causal,
                    late[:ROWS] - half_turn(late[ROWS:]),
                    early[:ROWS, :MEM] - early[ROWS:, MEM:],
                ),
                jnp.where(
                    causal,
                    late[ROWS:] + half_turn(late[:ROWS]),
                    early[ROWS:, :MEM] + early[:ROWS, MEM:],
                ),
            )
            for c in range(2):
                result[c, k] = quadrature * collide[c]
        return carry

    def advance(q, carry):
        for n in range(len(loads)):
            load(n, q).wait()
        for i in range(KB):
            k = q * KB + i
            collide = result[0, k], result[1, k]
            half = 0.5 * step_size
            if first:
                energy = energies[pl.ds(k, 1), :]
                xr, xi = base[0, k], base[1, k]
                fr = energy * xi + collide[1]
                fi = -(energy * xr + collide[0])
                value = (xr + step_size * fr, xi + step_size * fi)
                result[0, k] = xr + half * (fr + energy * value[1])
                result[1, k] = xi + half * (fi - energy * value[0])
            else:
                value = (base[0, k] + half * collide[1], base[1, k] - half * collide[0])
                for c in range(2):
                    result[c, k] = turn_over(value[c]) if last else value[c]
            if not last:
                for c in range(2):
                    turned[c, pl.ds(k, ROWS, stride=PITCH), :] = value[c]
        for n in range(len(saves)):
            save(n, q).start()
        return carry

    lax.fori_loop(0, STEPS, step, 0)
    lax.fori_loop(0, STEPS, advance, 0)
    if not last:
        for q in range(STEPS):
            pack_chunk(turned, block, q)
            chunk_copy(block, chunk, chunk_sem, q).start()
        emit(turned, mine, low)
        for q in range(STEPS):
            chunk_copy(block, chunk, chunk_sem, q).wait()
    for q in range(STEPS):
        for n in range(len(saves)):
            save(n, q).wait()


def stage(first, last, energies, sigma, own, own_low, near, far, base):
    state = pltpu.VMEM(STATE, F32)
    scratch = [state, state, pltpu.VMEM((2, (ROWS + 1) * PITCH, MEM), F32)]
    scratch += [pltpu.SemaphoreType.DMA((2, STEPS))]
    out_shape, spaces = [WIDE], [HBM]
    if not last:
        out_shape += EMITTED
        spaces += [VMEM, VMEM, HBM]
        scratch += emitting()[2:] + [pltpu.SemaphoreType.DMA((STEPS,))]

    def kernel(*refs):
        stage_kernel(first, last, *refs)

    operands = [sigma, own, own_low, near, far, pltpu.with_memory_space_constraint(base, pltpu.HBM)]
    in_specs = [VMEM] * 5 + [HBM]
    if first:
        operands.append(energies)
        in_specs.append(VMEM)
    return pl.pallas_call(
        kernel,
        in_specs=in_specs,
        out_specs=spaces,
        out_shape=out_shape,
        scratch_shapes=scratch,
        compiler_params=params(16),
        name="stage",
    )(*operands)


def from_behind(block, distance):
    count = lax.axis_size("ta")
    return lax.ppermute(block, "ta", [(i - distance, i) for i in range(distance, count)])


def exchange(block):
    return lax.all_to_all(block, "ka", split_axis=0, concat_axis=0, tiled=True)


def on_device(green, energies, reach):
    table = tables(K)
    time = lax.axis_index("ka") * PART + lax.broadcasted_iota(jnp.int32, (PART, MEM), 0)
    lag = (time - lax.broadcasted_iota(jnp.int32, (PART, MEM), 1)) & (MEM - 1)
    mine = lax.dynamic_slice_in_dim(reach, lax.axis_index("ka") * PART, PART)
    keep = (lag < mine[:, None]).astype(F32)

    energies = jnp.broadcast_to(energies[:, None], (OWN, MEM))

    def inputs(own, low, chunk):
        spread = exchange(chunk)
        near = from_behind(own, 1)
        far = from_behind(low, 2)
        sigma = self_energy(keep, table, spread)
        sigma = exchange(sigma)
        return sigma, own, low, near, far

    x, *rest = prepare(green)
    for counter in range(2):
        ahead, *rest = stage(True, False, energies, *inputs(*rest), x)
        last = counter == 1
        x, *rest = stage(False, last, energies, *inputs(*rest), ahead)
    return x


def solution(mesh):
    in_specs = (P(None, "ka", "ta", None), P("ka"), P("ta"))
    out_specs = P(None, "ka", "ta", None)
    return jax.shard_map(
        on_device, mesh=mesh, in_specs=in_specs, out_specs=out_specs, check_vma=False
    )
```

```python
import jax
import jax.numpy as jnp
import numpy as np
from jax import lax
from jax.experimental import pallas as pl
from jax.experimental.pallas import tpu as pltpu
from jax.sharding import PartitionSpec as P


K = 256
MEM = 128
ROWS = 64
OWN = 16
GROUP = 16
PART = 4
PITCH = 17
KB = 8
STEPS = OWN // KB
MIB = 2**20

quadrature = 0.0625
step_size = 0.25

F32 = jnp.float32
BF16 = jnp.bfloat16


def tables(count):
    numbers = np.arange(count)
    phase = (numbers[:, None] * numbers[None, :] % count) * (2.0 * np.pi / count)
    both = np.concatenate([np.cos(phase), np.sin(phase)], 0) / np.sqrt(count)
    return jnp.asarray(both.astype(np.float32).astype(jnp.bfloat16))


def grids():
    row = lax.broadcasted_iota(jnp.int32, (ROWS, MEM), 0)
    lane = lax.broadcasted_iota(jnp.int32, (ROWS, MEM), 1)
    return row, lane


def turn_over(block):
    row, lane = grids()
    index = (row - lane) & (MEM - 1)
    pieces = [
        jnp.take_along_axis(block[i : i + 8], index[i : i + 8], axis=1) for i in range(0, ROWS, 8)
    ]
    return jnp.concatenate(pieces, 0)


def half_turn(block):
    return pltpu.roll(block, MEM // 2, 1)


def self_energy_kernel(keep, table, x, out, y, sems):
    def save(pair):
        here = pl.ds(2 * pair, 2)
        return pltpu.make_async_copy(y.at[:, :, here], out.at[:, :, here], sems.at[pair])

    cosines, sines = table[:K], table[K:]
    forward = jnp.concatenate(
        [
            jnp.concatenate([cosines, -sines], 1),
            jnp.concatenate([sines, cosines], 1),
        ],
        0,
    )
    inverse = jnp.concatenate(
        [
            jnp.concatenate([cosines, sines], 1),
            jnp.concatenate([-sines, cosines], 1),
        ],
        0,
    )
    for pair in range(2):
        rows = []
        for part in range(2):
            sides = [x[:, part, 2 * pair + i].reshape(K, MEM) for i in range(2)]
            rows.append(jnp.concatenate(sides, 1))
        field = jnp.dot(forward, jnp.concatenate(rows, 0), preferred_element_type=F32)
        re, im = field[:K], field[K:]
        weight = -(re * re + im * im)
        z = jnp.concatenate([(weight * re).astype(BF16), (weight * im).astype(BF16)], 0)
        both = jnp.dot(inverse, z, preferred_element_type=F32)
        sigma = both[:K], both[K:]
        for part in range(2):
            for i in range(2):
                side = sigma[part][:, i * MEM : (i + 1) * MEM]
                kept = keep[2 * pair + i : 2 * pair + i + 1, :] > 0
                side = jnp.where(kept, side, 0.0).astype(BF16)
                y[:, part, 2 * pair + i] = side.reshape(GROUP, OWN, MEM)
        save(pair).start()
    for pair in range(2):
        save(pair).wait()


CHUNK = (GROUP, 2, PART, OWN, MEM)
STATE = (2, OWN, ROWS, MEM)
FAR = (OWN, ROWS, MEM)
HBM = pl.BlockSpec(memory_space=pltpu.HBM)
VMEM = pl.BlockSpec(memory_space=pltpu.VMEM)


def params(mib):
    return pltpu.CompilerParams(vmem_limit_bytes=int(mib * MIB))


def self_energy(keep, table, spread):
    return pl.pallas_call(
        self_energy_kernel,
        in_specs=[VMEM, VMEM, VMEM],
        out_specs=HBM,
        out_shape=pltpu.HBM(CHUNK, BF16),
        scratch_shapes=[pltpu.VMEM(CHUNK, BF16), pltpu.SemaphoreType.DMA((2,))],
        compiler_params=params(12),
        name="self_energy",
    )(keep, table, spread)


def piece(ref, q, size):
    here = pl.ds(q * size, size)
    return ref.at[here] if len(ref.shape) == 3 else ref.at[:, here]


def mover(pairs, sems, first, size=KB):
    def move(n, q):
        source, target = pairs[n]
        return pltpu.make_async_copy(piece(source, q, size), piece(target, q, size), sems.at[first + n, q])

    return move


def chunk_copy(block, chunk, sems, q):
    here = pl.ds(q * (GROUP // STEPS), GROUP // STEPS)
    return pltpu.make_async_copy(block.at[here], chunk.at[here], sems.at[q])


def pack_chunk(turned, block, q):
    for d in range(q * (GROUP // STEPS), (q + 1) * (GROUP // STEPS)):
        for c in range(2):
            for j in range(PART):
                t = (d * PART + j) * PITCH
                block[d, c, j] = turned[c, t : t + OWN, :].astype(BF16)


def emit(turned, near, far):
    row, lane = grids()
    causal = lane <= row

    def step(q, carry):
        for i in range(4):
            k = q * 4 + i
            low = []
            for c in range(2):
                value = turned[c, pl.ds(k, ROWS, stride=PITCH), :].astype(BF16)
                near[c, k] = value
                low.append(jnp.where(causal, value, jnp.zeros_like(value)))
            far[k] = jnp.where(lane < ROWS, low[0], half_turn(low[1]))
        return carry

    lax.fori_loop(0, OWN // 4, step, 0)


def prepare_kernel(x_in, out, near, far, chunk, x, y, turned, block, sems, sem):
    load = mover([(x_in, x)], sems, 0)
    save = mover([(y, out)], sems, 1)
    for q in range(STEPS):
        load(0, q).start()

    def step(q, carry):
        load(0, q).wait()
        for i in range(KB):
            k = q * KB + i
            for c in range(2):
                value = turn_over(x[c, k])
                y[c, k] = value
                turned[c, pl.ds(k, ROWS, stride=PITCH), :] = value
        save(0, q).start()
        return carry

    lax.fori_loop(0, STEPS, step, 0)
    for q in range(STEPS):
        pack_chunk(turned, block, q)
        chunk_copy(block, chunk, sem, q).start()
    emit(turned, near, far)
    for q in range(STEPS):
        chunk_copy(block, chunk, sem, q).wait()
        save(0, q).wait()


WIDE = pltpu.HBM(STATE, F32)
EMITTED = [pltpu.VMEM(STATE, BF16), pltpu.VMEM(FAR, BF16), pltpu.HBM(CHUNK, BF16)]


def emitting():
    return [
        pltpu.VMEM(STATE, BF16),
        pltpu.VMEM(FAR, BF16),
        pltpu.VMEM((2, (ROWS + 1) * PITCH, MEM), F32),
        pltpu.VMEM(CHUNK, BF16),
    ]


def prepare(x):
    scratch = pltpu.VMEM(STATE, F32)
    return pl.pallas_call(
        prepare_kernel,
        in_specs=[HBM],
        out_specs=[HBM, VMEM, VMEM, HBM],
        out_shape=[WIDE] + EMITTED,
        scratch_shapes=[scratch, scratch]
        + emitting()[2:]
        + [pltpu.SemaphoreType.DMA((2, STEPS)), pltpu.SemaphoreType.DMA((STEPS,))],
        compiler_params=params(16),
        name="prepare",
    )(pltpu.with_memory_space_constraint(x, pltpu.HBM))


def stage_kernel(first, last, *refs):
    refs = list(refs)
    sigma, own, own_low, near, far, base_in = refs[:6]
    refs = refs[6:]
    energies = refs.pop(0) if first else None
    if last:
        out, base, result, held, sems = refs
    else:
        out, mine, low, chunk, base, result, held, sems, turned, block, chunk_sem = refs

    loads = [(base_in, base)]
    saves = [(result, out)]
    load = mover(loads, sems, 0)
    save = mover(saves, sems, len(loads))
    for q in range(STEPS):
        for n in range(len(loads)):
            load(n, q).start()

    for d in range(GROUP):
        for c in range(2):
            for j in range(PART):
                t = d * PART + j
                held[c, t * PITCH : t * PITCH + OWN, :] = sigma[d, c, j].astype(F32)

    row, lane = grids()
    causal = lane <= row
    own_side = causal | (lane >= ROWS)
    seen = lane <= row + ROWS
    lower = lane < ROWS

    def only(kept, block):
        return jnp.where(kept, block, jnp.zeros_like(block))

    def step(q, carry):
        for i in range(KB):
            k = q * KB + i
            left = []
            for c in range(2):
                memory = held[c, pl.ds(k, ROWS, stride=PITCH), :].astype(BF16)
                inner = only(own_side, memory)
                outer = only(~own_side, memory)
                left.append(jnp.concatenate([inner, outer[:, :ROWS]], 1))
            left = jnp.concatenate(left, 0)
            packed = far[k]
            away = (packed, half_turn(packed))
            sides = []
            for c in range(2):
                rows = [
                    only(~causal, own[c, k]),
                    only(seen, half_turn(near[c, k])),
                    only(lower, away[c]),
                ]
                sides.append(jnp.concatenate(rows, 0))
            early = jnp.dot(left, jnp.concatenate(sides, 1), preferred_element_type=F32)
            late = jnp.dot(left[:, :ROWS], own_low[k], preferred_element_type=F32)
            collide = (
                jnp.where(
                    causal,
                    late[:ROWS] - half_turn(late[ROWS:]),
                    early[:ROWS, :MEM] - early[ROWS:, MEM:],
                ),
                jnp.where(
                    causal,
                    late[ROWS:] + half_turn(late[:ROWS]),
                    early[ROWS:, :MEM] + early[:ROWS, MEM:],
                ),
            )
            for c in range(2):
                result[c, k] = quadrature * collide[c]
        return carry

    def advance(q, carry):
        for n in range(len(loads)):
            load(n, q).wait()
        for i in range(KB):
            k = q * KB + i
            collide = result[0, k], result[1, k]
            half = 0.5 * step_size
            if first:
                energy = energies[pl.ds(k, 1), :]
                xr, xi = base[0, k], base[1, k]
                fr = energy * xi + collide[1]
                fi = -(energy * xr + collide[0])
                value = (xr + step_size * fr, xi + step_size * fi)
                result[0, k] = xr + half * (fr + energy * value[1])
                result[1, k] = xi + half * (fi - energy * value[0])
            else:
                value = (base[0, k] + half * collide[1], base[1, k] - half * collide[0])
                for c in range(2):
                    result[c, k] = turn_over(value[c]) if last else value[c]
            if not last:
                for c in range(2):
                    turned[c, pl.ds(k, ROWS, stride=PITCH), :] = value[c]
        for n in range(len(saves)):
            save(n, q).start()
        return carry

    lax.fori_loop(0, STEPS, step, 0)
    lax.fori_loop(0, STEPS, advance, 0)
    if not last:
        for q in range(STEPS):
            pack_chunk(turned, block, q)
            chunk_copy(block, chunk, chunk_sem, q).start()
        emit(turned, mine, low)
        for q in range(STEPS):
            chunk_copy(block, chunk, chunk_sem, q).wait()
    for q in range(STEPS):
        for n in range(len(saves)):
            save(n, q).wait()


def stage(first, last, energies, sigma, own, own_low, near, far, base):
    state = pltpu.VMEM(STATE, F32)
    scratch = [state, state, pltpu.VMEM((2, (ROWS + 1) * PITCH, MEM), F32)]
    scratch += [pltpu.SemaphoreType.DMA((2, STEPS))]
    out_shape, spaces = [WIDE], [HBM]
    if not last:
        out_shape += EMITTED
        spaces += [VMEM, VMEM, HBM]
        scratch += emitting()[2:] + [pltpu.SemaphoreType.DMA((STEPS,))]

    def kernel(*refs):
        stage_kernel(first, last, *refs)

    operands = [sigma, own, own_low, near, far, pltpu.with_memory_space_constraint(base, pltpu.HBM)]
    in_specs = [VMEM] * 5 + [HBM]
    if first:
        operands.append(energies)
        in_specs.append(VMEM)
    return pl.pallas_call(
        kernel,
        in_specs=in_specs,
        out_specs=spaces,
        out_shape=out_shape,
        scratch_shapes=scratch,
        compiler_params=params(16),
        name="stage",
    )(*operands)


def from_behind(block, distance):
    count = lax.axis_size("ta")
    return lax.ppermute(block, "ta", [(i - distance, i) for i in range(distance, count)])


def exchange(block):
    return lax.all_to_all(block, "ka", split_axis=0, concat_axis=0, tiled=True)


def on_device(green, energies, reach):
    table = tables(K)
    time = lax.axis_index("ka") * PART + lax.broadcasted_iota(jnp.int32, (PART, MEM), 0)
    lag = (time - lax.broadcasted_iota(jnp.int32, (PART, MEM), 1)) & (MEM - 1)
    mine = lax.dynamic_slice_in_dim(reach, lax.axis_index("ka") * PART, PART)
    keep = (lag < mine[:, None]).astype(F32)

    energies = jnp.broadcast_to(energies[:, None], (OWN, MEM))

    def inputs(own, low, chunk):
        spread = exchange(chunk)
        near = from_behind(own, 1)
        far = from_behind(low, 2)
        sigma = self_energy(keep, table, spread)
        sigma = exchange(sigma)
        return sigma, own, low, near, far

    x, *rest = prepare(green)
    for counter in range(2):
        ahead, *rest = stage(True, False, energies, *inputs(*rest), x)
        last = counter == 1
        x, *rest = stage(False, last, energies, *inputs(*rest), ahead)
    return x


def solution(mesh):
    in_specs = (P(None, "ka", "ta", None), P("ka"), P("ta"))
    out_specs = P(None, "ka", "ta", None)
    return jax.shard_map(
        on_device, mesh=mesh, in_specs=in_specs, out_specs=out_specs, check_vma=False
    )
```
